768 devices in a mesh: gx: 16 (over z_hi, y), gy: 48 (over z_lo, x, core).
Axes of the slice: x: 4, y: 8, z: 12 (z_hi: 2, z_lo: 6; z = z_hi * 6 + z_lo), core: 2. Of those that a mesh axis runs over, the one named last changes fastest.
Arguments:
- params: bfloat16 [768, 32, 192, 128], P(None, 'gx', 'gy'), may hold values from -6 to 6
- predicted: float32 [16, 48, 768, 128], P('gx', 'gy'), may hold values from -6 to 6
- measured_value: float32 [16, 48, 128], P('gx', 'gy'), may hold values from -6 to 6
- measurement_variance: float32 [16, 48, 128], P('gx', 'gy'), may hold values from 0.25 to 1
- observation_jitter: float32 [16, 48, 768, 128], P('gx', 'gy'), may hold values from -6 to 6
- obs_block: int32 [16, 48, 128], replicated, may hold values from 0 to 7
- taper_radius: int32 [32, 192], P('gx', 'gy'), may hold values from 1 to 2
- taper_pattern: int32 [32, 192, 25], P('gx', 'gy'), may hold values 0 or 1
Outputs:
- updated: bfloat16 [768, 32, 192, 128], P('gy', 'gx')
The draws below stay inside these ranges and needn't reach their ends.
All inputs are finite; a program needn't handle non-finite values. No bound on the sum of `taper_pattern` on one device may be relied on, other than what follows from the above.
Results may differ from the reference program's by a relative error of at most 0.0039.
Values may be sent and summed in bfloat16 or wider, within the bound.
A program may use at most 32 MiB of HBM per device.

```python
import math
import jax
import jax.numpy as jnp
from jax import lax

CELLS = 128
BLK_X = 2
BLK_Y = 4
OBS_TILE = 128
PATTERN = 25
MEMBERS = 768
NGX = 16
NGY = 48
NBX = 32
NBY = 192


def set_ends(drawn, key, least, top_value):
    longest = drawn.shape.index(max(drawn.shape))
    spots = []
    for shift in (0, 1):
        where = [jax.random.randint(jax.random.fold_in(key, axis), (), 0, length) for axis, length in enumerate(drawn.shape)]
        where[longest] = (where[longest] + shift) % drawn.shape[longest]
        spots.append(tuple(where))
    return drawn.at[spots[0]].set(least).at[spots[1]].set(top_value)


def levels(rng, shape, shards, low, top_value):
    level, own = 1.0, jax.random.fold_in(rng, 6)
    for dim, parts in shards:
        draws = jnp.exp(jax.random.uniform(jax.random.fold_in(own, dim), (parts,), jnp.float32, low / len(shards), top_value / len(shards)))
        level = level * jnp.repeat(draws, shape[dim] // parts).reshape([-1 if axis == dim else 1 for axis in range(len(shape))])
    return level


def normal_values(own_key, shape, scale, limit, pieces=(), held_as=jnp.bfloat16):
    entries = jax.random.normal(own_key, shape, jnp.float32) * scale
    if len(pieces) > 0:
        entries = levels(own_key, shape, pieces, -0.22, 0.18) * entries
    return jnp.clip(entries, min=-limit, max=limit).astype(held_as)


def setup_inputs(seed: int = 0) -> dict:
    splits = jax.random.split(jax.random.key(seed), 9)
    params = normal_values(splits[0], (MEMBERS, NBX, NBY, CELLS), 1.0, 6.0, ((1, 16), (2, 48)))
    predicted = normal_values(splits[1], (NGX, NGY, MEMBERS, OBS_TILE), 1.0, 6.0, ((0, 16), (1, 48)), jnp.float32)
    measured_value = normal_values(splits[2], (NGX, NGY, OBS_TILE), 1.0, 6.0, ((0, 16), (1, 48)), jnp.float32)
    measurement_variance = jnp.clip(jnp.exp(math.log(1.0) - 1.3862944 * jax.random.uniform(splits[3], (NGX, NGY, OBS_TILE), jnp.float32) ** levels(splits[3], (NGX, NGY, OBS_TILE), ((0, 16), (1, 48)), -0.2, 0.2)), 0.25, 1.0)
    observation_jitter = normal_values(splits[4], (NGX, NGY, MEMBERS, OBS_TILE), 1.0, 6.0, ((0, 16), (1, 48)), jnp.float32)
    obs_block = set_ends(jax.random.randint(splits[5], (NGX, NGY, OBS_TILE), 0, BLK_X * BLK_Y), jax.random.fold_in(splits[5], 1), 0, (BLK_X * BLK_Y) - 1).astype(jnp.int32)
    taper_radius = set_ends(jax.random.randint(splits[6], (NBX, NBY), 1, 3), jax.random.fold_in(splits[6], 1), 1, 2).astype(jnp.int32)
    taper_pattern = set_ends((jax.random.randint(splits[7], (NBX, NBY, PATTERN), 0, 4) < 3).astype(jnp.int32), jax.random.fold_in(splits[7], 1), 0, 1)
    return dict(params=params, predicted=predicted, measured_value=measured_value, measurement_variance=measurement_variance, observation_jitter=observation_jitter, obs_block=obs_block, taper_radius=taper_radius, taper_pattern=taper_pattern)


def tapers(radius, pattern, own_x, own_y, obs_x, obs_y):
    step_x = obs_x[None, :] - own_x[:, None]
    step_y = obs_y[None, :] - own_y[:, None]
    inside = (jnp.abs(step_x) <= 2) & (jnp.abs(step_y) <= 2)
    offset = (step_x + 2) * 5 + (step_y + 2)
    slots = jnp.arange(PATTERN, dtype=jnp.int32)
    picked = lax.optimization_barrier(jnp.sum(jnp.where(offset[:, :, None] == slots, pattern[:, None, :], 0), axis=2))
    reach = (radius + 1).astype(jnp.float32)
    spread = (step_x * step_x + step_y * step_y).astype(jnp.float32)
    shaped = jnp.maximum(1.0 - spread / (reach * reach)[:, None], 0.0)
    return jnp.where(inside, picked.astype(jnp.float32), 0.0) * shaped

def obs_places(obs_map, tiles_x, tiles_y):
    place_x = tiles_x[:, None, None] * BLK_X + obs_map // BLK_Y
    place_y = tiles_y[None, :, None] * BLK_Y + obs_map % BLK_Y
    return (place_x.reshape(-1), place_y.reshape(-1))

def contribution(anomaly, d_set, z_set, obs_map, tiles_x, tiles_y, own_x, own_y, radius, pattern):
    members = anomaly.shape[0]
    blocks = own_x.shape[0]
    place_x, place_y = obs_places(obs_map, tiles_x, tiles_y)
    weights = tapers(radius, pattern, own_x, own_y, place_x, place_y) / (members - 1)
    cross = lax.dot_general(anomaly.astype(jnp.float32), d_set.astype(jnp.float32), (((0,), (2,)), ((), ())), preferred_element_type=jnp.float32)
    complete_extent = cross.shape
    gain = (cross.reshape(blocks, -1, weights.shape[1]) * weights[:, None, :]).reshape(complete_extent).astype(jnp.bfloat16)
    return lax.dot_general(z_set.astype(jnp.float32), gain.astype(jnp.float32), (((0, 1, 3), (1, 2, 3)), ((), ())), preferred_element_type=jnp.float32)

def weigh(d_tile, observation_residual, variance, obs_map):
    members = d_tile.shape[0]
    gram = jnp.dot(d_tile.T.astype(jnp.float32), d_tile.astype(jnp.float32), preferred_element_type=jnp.float32) / (members - 1)
    same = obs_map[:, None] == obs_map[None, :]
    system = jnp.where(same, gram, 0.0) + jnp.diag(variance)
    factor = jnp.linalg.cholesky(system)
    solved = jax.scipy.linalg.cho_solve((factor, True), observation_residual.T)
    return solved.T.astype(jnp.bfloat16)

def weigh_packed(packed):
    return weigh(packed[0], packed[1], packed[2], packed[3])

def reference(params, predicted, measured_value, measurement_variance, observation_jitter, obs_block, taper_radius, taper_pattern):
    members = params.shape[0]
    blocks = BLK_X * BLK_Y
    tiles = NGX * NGY
    predicted_deviation = (predicted - lax.optimization_barrier(jnp.mean(predicted, axis=2, keepdims=True))).astype(jnp.bfloat16)
    observation_residual = measured_value[:, :, None, :] + jnp.sqrt(measurement_variance)[:, :, None, :] * observation_jitter - predicted
    weighted = lax.map(weigh_packed, (predicted_deviation.reshape(tiles, members, OBS_TILE), observation_residual.reshape(tiles, members, OBS_TILE), measurement_variance.reshape(tiles, OBS_TILE), obs_block.reshape(tiles, OBS_TILE)))
    weighted = weighted.reshape(NGX, NGY, members, OBS_TILE)
    stacked = jnp.stack([predicted_deviation, weighted], axis=2)
    padded = jnp.pad(stacked, ((1, 1), (1, 1), (0, 0), (0, 0), (0, 0)))
    map_pad = jnp.pad(obs_block, ((1, 1), (1, 1), (0, 0)))
    adjacent_everything = jnp.arange(3, dtype=jnp.int32) - 1
    local_ids = jnp.arange(blocks, dtype=jnp.int32)

    def per_tile(index):
        tile_x = (index // NGY).astype(jnp.int32)
        tile_y = (index % NGY).astype(jnp.int32)
        zero = jnp.int32(0)
        near = lax.dynamic_slice(padded, (tile_x, tile_y, zero, zero, zero), (3, 3, 2, members, OBS_TILE))
        near_map = lax.dynamic_slice(map_pad, (tile_x, tile_y, zero), (3, 3, OBS_TILE))
        start_x = (tile_x * BLK_X).astype(jnp.int32)
        start_y = (tile_y * BLK_Y).astype(jnp.int32)
        own_params = lax.dynamic_slice(params, (zero, start_x, start_y, zero), (members, BLK_X, BLK_Y, CELLS))
        wide = own_params.astype(jnp.float32)
        anomaly = (wide - lax.optimization_barrier(jnp.mean(wide, axis=0, keepdims=True))).astype(jnp.bfloat16).reshape(members, blocks * CELLS)
        radius = lax.dynamic_slice(taper_radius, (start_x, start_y), (BLK_X, BLK_Y)).reshape(blocks)
        pattern = lax.dynamic_slice(taper_pattern, (start_x, start_y, zero), (BLK_X, BLK_Y, PATTERN)).reshape(blocks, PATTERN)
        own_x = start_x + local_ids // BLK_Y
        own_y = start_y + local_ids % BLK_Y
        delta = contribution(anomaly, near[:, :, 0], near[:, :, 1], near_map, tile_x + adjacent_everything, tile_y + adjacent_everything, own_x, own_y, radius, pattern)
        return (wide + delta.reshape(members, BLK_X, BLK_Y, CELLS)).astype(jnp.bfloat16)
    updated = lax.map(per_tile, jnp.arange(tiles, dtype=jnp.int32))
    updated = updated.reshape(NGX, NGY, members, BLK_X, BLK_Y, CELLS).transpose(2, 0, 3, 1, 4, 5)
    return updated.reshape(members, NGX * BLK_X, NGY * BLK_Y, CELLS)
```

```python
import functools

import jax
import jax.numpy as jnp
from jax import lax
from jax.experimental import pallas as pl
from jax.experimental.pallas import tpu as pltpu
from jax.sharding import PartitionSpec as P

CELLS = 128
BLK_X = 2
BLK_Y = 4
OBS = 128
PATTERN = 25
BLOCKS = BLK_X * BLK_Y
TILES = 9
CENTRE = 4
NEWTON = 9
MESH = pl.DeviceIdType.MESH
EXACT = lax.Precision.HIGHEST


def taper_table(near_map, radius, pattern):
    tile = jnp.arange(TILES, dtype=jnp.int32)
    obs_x = ((tile // 3 - 1) * BLK_X)[:, None] + near_map // BLK_Y
    obs_y = ((tile % 3 - 1) * BLK_Y)[:, None] + near_map % BLK_Y
    own = jnp.arange(BLOCKS, dtype=jnp.int32)
    step_x = obs_x.reshape(1, -1) - (own // BLK_Y)[:, None]
    step_y = obs_y.reshape(1, -1) - (own % BLK_Y)[:, None]
    inside = (jnp.abs(step_x) <= 2) & (jnp.abs(step_y) <= 2)
    offset = (step_x + 2) * 5 + (step_y + 2)
    slots = jnp.arange(PATTERN, dtype=jnp.int32)
    picked = jnp.sum(jnp.where(offset[:, :, None] == slots, pattern[:, None, :], 0), axis=2)
    reach = (radius + 1).astype(jnp.float32)
    spread = (step_x * step_x + step_y * step_y).astype(jnp.float32)
    shaped = jnp.maximum(1.0 - spread / (reach * reach)[:, None], 0.0)
    return jnp.where(inside, picked.astype(jnp.float32), 0.0) * shaped


def inverse(system, least):
    size = system.shape[0]
    most = jnp.max(jnp.sum(jnp.abs(system), axis=0, keepdims=True), axis=1, keepdims=True)
    scale = 2.0 / (most + least)
    spread = (most - least) / (most + least)
    eye = (
        lax.broadcasted_iota(jnp.int32, (size, size), 0)
        == lax.broadcasted_iota(jnp.int32, (size, size), 1)
    )
    inv = jnp.where(eye, 2.0 * scale, 0.0) - (scale * scale) * system
    for _ in range(NEWTON):
        square = spread * spread
        scale = 2.0 / (2.0 - square)
        spread = square / (2.0 - square)
        turned = jnp.dot(system, inv, precision=EXACT, preferred_element_type=jnp.float32)
        step = jnp.dot(inv, turned, precision=EXACT, preferred_element_type=jnp.float32)
        inv = (2.0 * scale) * inv - (scale * scale) * step
    return inv


def front_kernel(
    rows,
    cols,
    pred_ref,
    jitter_ref,
    value_ref,
    var_ref,
    map_row_ref,
    map_col_ref,
    taper_ref,
    params_ref,
    out_ref,
    d_ref,
    w_ref,
    gain_ref,
    anom_ref,
    send_sem,
    recv_sem,
):
    members = pred_ref.shape[0]
    gx = lax.axis_index("gx")
    gy = lax.axis_index("gy")
    has_up = gx > 0
    has_down = gx < rows - 1
    has_left = gy > 0
    has_right = gy < cols - 1
    barrier = pltpu.get_barrier_semaphore()

    def greet(there, dev):
        @pl.when(there)
        def _():
            pl.semaphore_signal(barrier, inc=1, device_id=dev, device_id_type=MESH)

    up, down, left, right = (gx - 1, gy), (gx + 1, gy), (gx, gy - 1), (gx, gy + 1)
    greet(has_up, up)
    greet(has_down, down)
    greet(has_left, left)
    greet(has_right, right)

    def moves(kind):
        first = [(0, CENTRE, 1, has_down, down), (1, CENTRE, 7, has_up, up)]
        own = [(2, CENTRE, 3, has_right, right), (3, CENTRE, 5, has_left, left)]
        passed = [
            (4, 1, 0, has_right, right),
            (5, 1, 2, has_left, left),
            (6, 7, 6, has_right, right),
            (7, 7, 8, has_left, left),
        ]
        return first, own, passed

    bufs = (d_ref, w_ref)

    def copy(kind, move):
        index, src, dst, _, dev = move
        return pltpu.make_async_remote_copy(
            src_ref=bufs[kind].at[src],
            dst_ref=bufs[kind].at[dst],
            send_sem=send_sem.at[kind, index],
            recv_sem=recv_sem.at[kind, dst],
            device_id=dev,
            device_id_type=MESH,
        )

    def start(kind, group):
        for move in group:

            @pl.when(move[3])
            def _(move=move):
                copy(kind, move).start()

    def wait_sent(kind):
        for group in moves(kind):
            for move in group:

                @pl.when(move[3])
                def _(move=move):
                    copy(kind, move).wait_send()

    arrives = {
        1: has_up,
        7: has_down,
        0: has_left,
        3: has_left,
        6: has_left,
        2: has_right,
        5: has_right,
        8: has_right,
    }

    def wait_arrived(kind, slots):
        for slot in slots:

            @pl.when(arrives[slot])
            def _(slot=slot):
                pltpu.make_async_copy(
                    bufs[kind].at[slot], bufs[kind].at[slot], recv_sem.at[kind, slot]
                ).wait()

    for slot, there in arrives.items():

        @pl.when(jnp.logical_not(there))
        def _(slot=slot):
            d_ref[slot] = jnp.zeros(d_ref.shape[1:], d_ref.dtype)
            w_ref[slot] = jnp.zeros(w_ref.shape[1:], w_ref.dtype)

    pred = pred_ref[...]
    deviation = pred - jnp.sum(pred, axis=0, keepdims=True) / members
    d_own = deviation.astype(jnp.bfloat16)
    d_turned = deviation.T.astype(jnp.bfloat16)
    d_ref[CENTRE] = d_turned
    near = (
        has_up.astype(jnp.int32)
        + has_down.astype(jnp.int32)
        + has_left.astype(jnp.int32)
        + has_right.astype(jnp.int32)
    )
    pl.semaphore_wait(barrier, near)
    first, own, passed = moves(0)
    start(0, first)
    start(0, own)

    gram = jnp.dot(d_turned, d_own, preferred_element_type=jnp.float32) / (members - 1)
    same = map_col_ref[...] == map_row_ref[...]
    eye = (
        lax.broadcasted_iota(jnp.int32, (OBS, OBS), 0)
        == lax.broadcasted_iota(jnp.int32, (OBS, OBS), 1)
    )
    variance = var_ref[...]
    system = jnp.where(same, gram, 0.0) + jnp.where(eye, variance, 0.0)
    inv = inverse(system, jnp.min(variance, axis=1, keepdims=True))
    residual = value_ref[...] + jnp.sqrt(variance) * jitter_ref[...] - pred_ref[...]
    w_ref[CENTRE] = jnp.dot(
        residual, inv, precision=EXACT, preferred_element_type=jnp.float32
    ).astype(jnp.bfloat16)
    start(1, first)
    start(1, own)
    wait_arrived(0, (1, 7))
    start(0, passed)

    for block in range(BLOCKS):
        cells = slice(block * CELLS, (block + 1) * CELLS)
        wide = params_ref[:, cells].astype(jnp.float32)
        mean = jnp.sum(wide, axis=0, keepdims=True) / members
        anom_ref[:, cells] = (wide - mean).astype(jnp.bfloat16)

    wait_arrived(1, (1, 7))
    start(1, passed)
    wait_arrived(0, (3, 5, 0, 2, 6, 8))

    def gain_of(tile):
        cross = jnp.dot(d_ref[tile], anom_ref[...], preferred_element_type=jnp.float32)
        rows_of = pl.ds(pl.multiple_of(tile * OBS, OBS), OBS)
        weight = taper_ref[rows_of, :]
        for block in range(BLOCKS):
            cells = slice(block * CELLS, (block + 1) * CELLS)
            gain_ref[rows_of, cells] = (cross[:, cells] * weight[:, block : block + 1]).astype(
                jnp.bfloat16
            )

    @pl.loop(0, TILES)
    def _(tile):
        gain_of(tile)

    wait_arrived(1, (3, 5, 0, 2, 6, 8))
    part = 256

    @pl.loop(0, members // part)
    def _(step):
        who = pl.ds(pl.multiple_of(step * part, part), part)
        lhs = jnp.concatenate([w_ref[tile, who, :] for tile in range(TILES)], axis=1)
        for chunk in range(BLOCKS // 2):
            cells = slice(chunk * 256, (chunk + 1) * 256)
            delta = jnp.dot(lhs, gain_ref[:, cells], preferred_element_type=jnp.float32)
            out_ref[who, cells] = (params_ref[who, cells].astype(jnp.float32) + delta).astype(
                jnp.bfloat16
            )

    wait_sent(0)
    wait_sent(1)


def front(rows, cols, pred, jitter, value, var, map_row, map_col, taper, params):
    members = pred.shape[0]
    vmem = pl.BlockSpec(memory_space=pltpu.VMEM)
    return pl.pallas_call(
        functools.partial(front_kernel, rows, cols),
        out_shape=jax.ShapeDtypeStruct(params.shape, jnp.bfloat16),
        in_specs=[vmem] * 8,
        out_specs=vmem,
        scratch_shapes=[
            pltpu.VMEM((TILES, OBS, members), jnp.bfloat16),
            pltpu.VMEM((TILES, members, OBS), jnp.bfloat16),
            pltpu.VMEM((TILES * OBS, BLOCKS * CELLS), jnp.bfloat16),
            pltpu.VMEM((members, BLOCKS * CELLS), jnp.bfloat16),
            pltpu.SemaphoreType.DMA((2, 8)),
            pltpu.SemaphoreType.DMA((2, TILES)),
        ],
        compiler_params=pltpu.CompilerParams(
            collective_id=0, has_side_effects=True, vmem_limit_bytes=40 << 20
        ),
    )(pred, jitter, value, var, map_row, map_col, taper, params)


def regroup_kernel(count, send_ref, recv_ref, own_sem, send_sem, recv_sem):
    gx = lax.axis_index("gx")
    me = lax.axis_index("gy")
    share = recv_ref.shape[1]
    barrier = pltpu.get_barrier_semaphore()

    def greet(step, carry):
        pl.semaphore_signal(
            barrier, inc=1, device_id=(gx, lax.rem(me + step, count)), device_id_type=MESH
        )
        return carry

    def rows_for(target):
        return send_ref.at[pl.ds(pl.multiple_of(target * share, share), share), :]

    lax.fori_loop(1, count, greet, 0)
    own = pltpu.make_async_copy(rows_for(me), recv_ref.at[me], own_sem)
    own.start()
    pl.semaphore_wait(barrier, count - 1)

    def send(step, carry):
        target = lax.rem(me + step, count)
        pltpu.make_async_remote_copy(
            src_ref=rows_for(target),
            dst_ref=recv_ref.at[me],
            send_sem=send_sem,
            recv_sem=recv_sem,
            device_id=(gx, target),
            device_id_type=MESH,
        ).start()
        return carry

    lax.fori_loop(1, count, send, 0)
    others = recv_ref.at[pl.ds(0, count - 1)]
    pltpu.make_async_copy(others, others, send_sem).wait()
    pltpu.make_async_copy(others, others, recv_sem).wait()
    own.wait()


def regroup(count, updated):
    members, cells = updated.shape
    vmem = pl.BlockSpec(memory_space=pltpu.VMEM)
    return pl.pallas_call(
        functools.partial(regroup_kernel, count),
        out_shape=jax.ShapeDtypeStruct((count, members // count, cells), updated.dtype),
        in_specs=[vmem],
        out_specs=vmem,
        scratch_shapes=[pltpu.SemaphoreType.DMA] * 3,
        compiler_params=pltpu.CompilerParams(collective_id=1, has_side_effects=True),
    )(updated)


def per_device(
    rows,
    cols,
    params,
    predicted,
    measured_value,
    measurement_variance,
    observation_jitter,
    obs_block,
    taper_radius,
    taper_pattern,
):
    members = params.shape[0]
    tile_x = lax.axis_index("gx")
    tile_y = lax.axis_index("gy")
    map_pad = jnp.pad(obs_block, ((1, 1), (1, 1), (0, 0)))
    near_map = lax.dynamic_slice(map_pad, (tile_x, tile_y, jnp.int32(0)), (3, 3, OBS)).reshape(
        TILES, OBS
    )
    taper = taper_table(
        near_map, taper_radius.reshape(BLOCKS), taper_pattern.reshape(BLOCKS, PATTERN)
    ) / (members - 1)
    own_map = near_map[CENTRE]
    updated = front(
        rows,
        cols,
        predicted[0, 0],
        observation_jitter[0, 0],
        measured_value[0],
        measurement_variance[0],
        own_map[None, :],
        own_map[:, None],
        taper.T,
        params.reshape(members, BLOCKS * CELLS),
    )
    regrouped = regroup(cols, updated)
    share = members // cols
    out = regrouped.reshape(cols, share, BLK_X, BLK_Y, CELLS).transpose(1, 2, 0, 3, 4)
    return out.reshape(share, BLK_X, cols * BLK_Y, CELLS)


def solution(mesh):
    placed = (
        P(None, "gx", "gy", None),
        P("gx", "gy", None, None),
        P("gx", "gy", None),
        P("gx", "gy", None),
        P("gx", "gy", None, None),
        P(),
        P("gx", "gy"),
        P("gx", "gy", None),
    )
    body = functools.partial(per_device, mesh.shape["gx"], mesh.shape["gy"])
    return jax.shard_map(
        body, mesh=mesh, in_specs=placed, out_specs=P("gy", "gx", None, None), check_vma=False
    )
```

```python
import functools

import jax
import jax.numpy as jnp
from jax import lax
from jax.experimental import pallas as pl
from jax.experimental.pallas import tpu as pltpu
from jax.sharding import PartitionSpec as P

CELLS = 128
BLK_X = 2
BLK_Y = 4
OBS = 128
PATTERN = 25
BLOCKS = BLK_X * BLK_Y
TILES = 9
UP, CENTRE, DOWN = 3, 4, 5
NEWTON = 9
PIECES = 6
ROUNDS = 3
MESH = pl.DeviceIdType.MESH
EXACT = lax.Precision.HIGHEST


def mm(a, b, precision=None):
    return jnp.dot(a, b, precision=precision, preferred_element_type=jnp.float32)


def newton_start(system, least):
    size = system.shape[0]
    most = jnp.max(jnp.sum(jnp.abs(system), axis=0, keepdims=True), axis=1, keepdims=True)
    scale = 2.0 / (most + least)
    spread = (most - least) / (most + least)
    eye = (
        lax.broadcasted_iota(jnp.int32, (size, size), 0)
        == lax.broadcasted_iota(jnp.int32, (size, size), 1)
    )
    return jnp.where(eye, 2.0 * scale, 0.0) - (scale * scale) * system, spread


def newton(system, inv, spread, steps):
    for _ in range(steps):
        square = spread * spread
        scale = 2.0 / (2.0 - square)
        spread = square / (2.0 - square)
        step = mm(inv, mm(system, inv, EXACT), EXACT)
        inv = (2.0 * scale) * inv - (scale * scale) * step
    return inv, spread


def kernel(
    rows,
    cols,
    radius_ref,
    pred_ref,
    jitter_ref,
    value_ref,
    var_ref,
    map_ref,
    pattern_ref,
    params_hbm,
    recv_ref,
    params_ref,
    d_ref,
    w_ref,
    gain_ref,
    anom_ref,
    wide_ref,
    delta_ref,
    taper_ref,
    sent_ref,
    d_near,
    d_far,
    w_near,
    w_far,
    load_sem,
    own_sem,
    all_send,
    all_recv,
    d_send,
    d_recv,
    w_send,
    w_recv,
    d_relay,
    w_relay,
):
    members = pred_ref.shape[0]
    piece = members // PIECES
    half = rows // 2
    share = members // cols
    gx = lax.axis_index("gx")
    gy = lax.axis_index("gy")
    lower = gx < half
    upper = gx >= half
    low_seam = gx == half - 1
    high_seam = gx == half
    seam = (gx == half - 1) | (gx == half)
    relay = jnp.logical_not(seam)
    column = lax.rem(gx, half)
    across = lax.rem(gx + half, rows)
    has_left = gy > 0
    has_right = gy < cols - 1
    sends_up = (gx > 0) & jnp.logical_not(high_seam)
    sends_down = (gx < rows - 1) & jnp.logical_not(low_seam)

    params_load = pltpu.make_async_copy(params_hbm, params_ref, load_sem)
    params_load.start()

    barrier = pltpu.get_barrier_semaphore()

    def greet(dev):
        pl.semaphore_signal(barrier, inc=1, device_id=dev, device_id_type=MESH)

    def greet_group(step, carry):
        greet((gx, lax.rem(gy + step, cols)))
        return carry

    lax.fori_loop(1, cols, greet_group, 0)
    greet((across, gy))

    @pl.when(sends_up)
    def _():
        greet((gx - 1, gy))

    @pl.when(sends_down)
    def _():
        greet((gx + 1, gy))

    for side, is_side, is_seam, at in (
        (0, lower, low_seam, half - 1),
        (half, upper, high_seam, half),
    ):

        @pl.when(is_side & relay)
        def _(at=at):
            greet((at, gy))

        @pl.when(is_seam)
        def _(side=side, at=at):
            for target in range(side, side + half):
                if target != at:
                    greet((target, gy))

    greetings = (
        cols
        + sends_up.astype(jnp.int32)
        + sends_down.astype(jnp.int32)
        + 1
        + (half - 2) * seam.astype(jnp.int32)
    )

    def remote(src, dst, send, recv, dev):
        return pltpu.make_async_remote_copy(
            src_ref=src,
            dst_ref=dst,
            send_sem=send,
            recv_sem=recv,
            device_id=dev,
            device_id_type=MESH,
        )

    class Parcel:
        def __init__(self, buf, start, size, near, far, send, recv, relays):
            self.buf, self.start, self.size = buf, start, size
            self.near, self.far, self.send, self.recv, self.relays = near, far, send, recv, relays
            self.part = size // half

        def rows_of(self, slot):
            return self.buf.at[slot, pl.ds(self.start, self.size), :]

        def part_of(self, slot, index):
            offset = pl.multiple_of(self.start + index * self.part, self.part)
            return self.buf.at[slot, pl.ds(offset, self.part), :]

        def hop(self, index, src, dst, dev):
            return remote(
                self.rows_of(src), self.rows_of(dst), self.send.at[index], self.recv.at[dst], dev
            )

        def own_hops(self):
            return (
                (sends_down, self.hop(0, CENTRE, UP, (gx + 1, gy))),
                (sends_up, self.hop(1, CENTRE, DOWN, (gx - 1, gy))),
                (has_right, self.hop(2, CENTRE, 1, (gx, gy + 1))),
                (has_left, self.hop(3, CENTRE, 7, (gx, gy - 1))),
            )

        def passed_hops(self):
            return (
                (has_right, self.hop(4, UP, 0, (gx, gy + 1))),
                (has_left, self.hop(5, UP, 6, (gx, gy - 1))),
                (has_right, self.hop(6, DOWN, 2, (gx, gy + 1))),
                (has_left, self.hop(7, DOWN, 8, (gx, gy - 1))),
            )

        def seam_hops(self):
            hops = []
            for side, is_seam, at in ((0, low_seam, half - 1), (half, high_seam, half)):
                for index in range(half):
                    if side + index == at:
                        dst, recv, dev = self.far, self.relays.at[1], (across, gy)
                    else:
                        dst, recv, dev = self.near, self.relays.at[0], (side + index, gy)
                    src = self.part_of(CENTRE, index)
                    hops.append((is_seam, remote(src, dst, self.send.at[8 + index], recv, dev)))
            return hops

        def cross_hops(self):
            low_end, high_end = gx == 0, gx == rows - 1
            inner = relay & jnp.logical_not(low_end) & jnp.logical_not(high_end)
            send, dev = self.send.at[8], (across, gy)
            return (
                (inner, remote(self.near, self.far, send, self.relays.at[1], dev)),
                (low_end, remote(self.near, self.part_of(UP, 0), send, self.recv.at[UP], dev)),
                (
                    high_end,
                    remote(self.near, self.part_of(DOWN, half - 1), send, self.recv.at[DOWN], dev),
                ),
            )

        def last_hops(self):
            hops = []
            for is_side, at, slot in ((lower, half - 1, DOWN), (upper, half, UP)):
                dst = self.part_of(slot, column)
                hop = remote(self.far, dst, self.send.at[9], self.recv.at[slot], (at, gy))
                hops.append((is_side & relay, hop))
            return hops

        def wait_near(self):
            @pl.when(relay)
            def _():
                pltpu.make_async_copy(self.near, self.near, self.relays.at[0]).wait()

        def wait_far(self):
            @pl.when(relay)
            def _():
                pltpu.make_async_copy(self.far, self.far, self.relays.at[1]).wait()

        def wait_slots(self, slots, where=None):
            for slot in slots:
                there = arrives[slot] if where is None else arrives[slot] & where

                @pl.when(there)
                def _(slot=slot):
                    ref = self.rows_of(slot)
                    pltpu.make_async_copy(ref, ref, self.recv.at[slot]).wait()

        def start_own(self):
            start(self.own_hops())
            start(self.seam_hops())

        def cross(self):
            self.wait_near()
            start(self.cross_hops())

        def last(self):
            self.wait_far()
            start(self.last_hops())

        def pass_on(self, where):
            self.wait_slots((UP, DOWN), where)
            start(self.passed_hops(), where)

        def wait_sent(self):
            for hops in (
                self.own_hops(),
                self.passed_hops(),
                self.seam_hops(),
                self.cross_hops(),
                self.last_hops(),
            ):
                for there, hop in hops:

                    @pl.when(there)
                    def _(hop=hop):
                        hop.wait_send()

    def start(hops, where=None):
        for there, hop in hops:

            @pl.when(there if where is None else there & where)
            def _(hop=hop):
                hop.start()

    arrives = {UP: gx > 0, DOWN: gx < rows - 1}
    arrives.update({slot: has_left for slot in (0, 1, 2)})
    arrives.update({slot: has_right for slot in (6, 7, 8)})

    for slot, there in arrives.items():

        @pl.when(jnp.logical_not(there))
        def _(slot=slot):
            d_ref[slot] = jnp.zeros(d_ref.shape[1:], d_ref.dtype)
            w_ref[slot] = jnp.zeros(w_ref.shape[1:], w_ref.dtype)

    d_parcel = Parcel(d_ref, 0, OBS, d_near, d_far, d_send, d_recv, d_relay)
    w_parcels = [
        Parcel(
            w_ref,
            turn * 2 * piece,
            2 * piece,
            w_near.at[turn],
            w_far.at[turn],
            w_send.at[turn],
            w_recv.at[turn],
            w_relay.at[turn],
        )
        for turn in range(ROUNDS)
    ]

    pred = pred_ref[...]
    deviation = pred - jnp.sum(pred, axis=0, keepdims=True) / members
    d_own = deviation.astype(jnp.bfloat16)
    d_turned = deviation.T.astype(jnp.bfloat16)
    d_ref[CENTRE] = d_turned
    pl.semaphore_wait(barrier, greetings)
    d_parcel.start_own()

    gram = mm(d_turned, d_own) / (members - 1)
    own_map = jnp.broadcast_to(map_ref[gx, pl.ds(gy, 1), :].astype(jnp.float32), (OBS, OBS))
    eye = (
        lax.broadcasted_iota(jnp.int32, (OBS, OBS), 0)
        == lax.broadcasted_iota(jnp.int32, (OBS, OBS), 1)
    )
    variance = var_ref[...]
    system = jnp.where(own_map == own_map.T, gram, 0.0) + jnp.where(eye, variance, 0.0)
    inv, spread = newton_start(system, jnp.min(variance, axis=1, keepdims=True))
    inv, spread = newton(system, inv, spread, 4)
    d_parcel.cross()
    inv, spread = newton(system, inv, spread, NEWTON - 4)
    deviation_scale = jnp.sqrt(variance)
    for turn in range(ROUNDS):
        for place, which in enumerate((turn, PIECES - 1 - turn)):
            who = slice(which * piece, (which + 1) * piece)
            residual = (
                value_ref[...] + deviation_scale * jitter_ref[who, :] - pred_ref[who, :]
            )
            at = (2 * turn + place) * piece
            w_ref[CENTRE, at : at + piece, :] = mm(residual, inv, EXACT).astype(jnp.bfloat16)
        w_parcels[turn].start_own()

    d_parcel.pass_on(relay)
    d_parcel.last()

    block = lax.broadcasted_iota(jnp.int32, (BLOCKS, OBS), 0)
    reach = jnp.zeros((BLOCKS, OBS), jnp.int32)
    for index in range(BLOCKS):
        reach = jnp.where(block == index, radius_ref[index // BLK_Y, index % BLK_Y] + 1, reach)
    reach = reach.astype(jnp.float32)
    reach = reach * reach
    listed = [
        jnp.broadcast_to(pattern_ref[:, slot : slot + 1], (BLOCKS, OBS)) for slot in range(PATTERN)
    ]
    for tile in range(TILES):
        at_x = lax.rem(gx + rows + tile % 3 - 1, rows)
        at_y = lax.rem(gy + cols + tile // 3 - 1, cols)
        near = jnp.broadcast_to(map_ref[at_x, pl.ds(at_y, 1), :], (BLOCKS, OBS))
        step_x = (tile % 3 - 1) * BLK_X + (near >> 2) - (block >> 2)
        step_y = (tile // 3 - 1) * BLK_Y + (near & 3) - (block & 3)
        inside = (jnp.abs(step_x) <= 2) & (jnp.abs(step_y) <= 2)
        offset = (step_x + 2) * 5 + (step_y + 2)
        picked = jnp.zeros((BLOCKS, OBS), jnp.int32)
        for slot in range(PATTERN):
            picked = jnp.where(offset == slot, listed[slot], picked)
        distance = (step_x * step_x + step_y * step_y).astype(jnp.float32)
        shaped = jnp.maximum(1.0 - distance / reach, 0.0)
        taper = jnp.where(inside, picked.astype(jnp.float32), 0.0) * shaped / (members - 1)
        filled = jnp.concatenate([taper, jnp.zeros((OBS - BLOCKS, OBS), jnp.float32)], axis=0)
        taper_ref[tile * OBS : (tile + 1) * OBS, :] = filled.T

    params_load.wait()
    batch = 64

    def batch_rows(step):
        return pl.ds(pl.multiple_of(step * batch * BLOCKS, batch * BLOCKS), batch * BLOCKS)

    def batch_of(step):
        wide = params_ref[batch_rows(step), :].astype(jnp.float32)
        return wide.reshape(batch, BLOCKS, CELLS)

    mean = lax.fori_loop(
        0,
        members // batch,
        lambda step, total: total + jnp.sum(batch_of(step), axis=0),
        jnp.zeros((BLOCKS, CELLS), jnp.float32),
    ) * (1.0 / members)

    @pl.loop(0, members // batch)
    def _(step):
        centred = batch_of(step) - mean[None]
        wide_ref[batch_rows(step), :] = centred.reshape(batch * BLOCKS, CELLS)

    for index in range(BLOCKS):
        for first in range(0, members, 256):
            anom_ref[first : first + 256, index * CELLS : (index + 1) * CELLS] = wide_ref[
                pl.ds(first * BLOCKS + index, 256, stride=BLOCKS), :
            ].astype(jnp.bfloat16)

    near_tiles = 6
    obs = near_tiles * OBS

    def first_slot(group):
        return 3 * (group % 2)

    def gain_of(group):
        cells = slice(group * 2 * CELLS, (group + 1) * 2 * CELLS)
        first = first_slot(group)
        d_set = d_ref[first : first + near_tiles].reshape(obs, members)
        cross = mm(d_set, anom_ref[:, cells])
        weight = taper_ref[first * OBS : first * OBS + obs, :]
        for side in range(2):
            index = 2 * group + side
            gain_ref[group, :, side * CELLS : (side + 1) * CELLS] = (
                cross[:, side * CELLS : (side + 1) * CELLS] * weight[:, index : index + 1]
            ).astype(jnp.bfloat16)

    w_parcels[0].cross()
    w_parcels[0].pass_on(relay)
    w_parcels[1].cross()
    d_parcel.pass_on(seam)
    d_parcel.wait_slots((1, 7, 0, 2, 6, 8))
    gain_of(0)
    gain_of(1)
    w_parcels[0].last()
    w_parcels[1].pass_on(relay)
    w_parcels[2].cross()
    gain_of(2)
    gain_of(3)

    fan = cols // PIECES

    def send_rows(target):
        size = share * BLOCKS
        return sent_ref.at[pl.ds(pl.multiple_of(target * size, size), size), :]

    own_copy = pltpu.make_async_copy(send_rows(gy), recv_ref.at[gy], own_sem)
    far_side = lax.div(2 * gy, cols)

    def finish(turn):
        w_parcels[turn].pass_on(seam)
        w_parcels[turn].wait_slots((1, 7, 0, 2, 6, 8))
        who = slice(turn * 2 * piece, (turn + 1) * 2 * piece)
        for group in range(BLOCKS // 2):
            first = first_slot(group)
            w_set = jnp.concatenate(
                [w_ref[slot, who, :] for slot in range(first, first + near_tiles)], axis=1
            )
            delta = mm(w_set, gain_ref[group])
            for side in range(2):
                delta_ref[pl.ds(2 * group + side, 2 * piece, stride=BLOCKS), :] = delta[
                    :, side * CELLS : (side + 1) * CELLS
                ]
        size = piece * BLOCKS
        for place, which in enumerate((turn, PIECES - 1 - turn)):
            to = slice(which * size, (which + 1) * size)
            sent_ref[to, :] = (
                params_ref[to, :].astype(jnp.float32)
                + delta_ref[place * size : (place + 1) * size, :]
            ).astype(jnp.bfloat16)
        other, near = PIECES - 1 - turn, turn
        for which in (
            other + far_side * (near - other),
            near + far_side * (other - near),
        ):

            def send(step, carry, which=which):
                target = which * fan + lax.rem(step + gy, fan)

                @pl.when(target != gy)
                def _():
                    remote(
                        send_rows(target), recv_ref.at[gy], all_send, all_recv, (gx, target)
                    ).start()

                @pl.when(target == gy)
                def _():
                    own_copy.start()

                return carry

            lax.fori_loop(0, fan, send, 0)

    finish(0)
    w_parcels[1].last()
    w_parcels[2].pass_on(relay)
    finish(1)
    w_parcels[2].last()
    finish(2)

    others = recv_ref.at[pl.ds(0, cols - 1)]
    d_parcel.wait_sent()
    for parcel in w_parcels:
        parcel.wait_sent()
    own_copy.wait()
    pltpu.make_async_copy(others, others, all_send).wait()
    pltpu.make_async_copy(others, others, all_recv).wait()


def per_device(
    rows,
    cols,
    params,
    predicted,
    measured_value,
    measurement_variance,
    observation_jitter,
    obs_block,
    taper_radius,
    taper_pattern,
):
    members = params.shape[0]
    share = members // cols
    half = rows // 2
    cells = BLOCKS * CELLS
    turn = members // ROUNDS
    vmem = pl.BlockSpec(memory_space=pltpu.VMEM)
    smem = pl.BlockSpec(memory_space=pltpu.SMEM)
    anywhere = pl.BlockSpec(memory_space=pl.ANY)
    dma = pltpu.SemaphoreType.DMA
    bf16, f32 = jnp.bfloat16, jnp.float32
    regrouped = pl.pallas_call(
        functools.partial(kernel, rows, cols),
        out_shape=jax.ShapeDtypeStruct((cols, share * BLOCKS, CELLS), bf16),
        in_specs=[smem] + [vmem] * 6 + [anywhere],
        out_specs=anywhere,
        scratch_shapes=[
            pltpu.VMEM((members * BLOCKS, CELLS), bf16),
            pltpu.VMEM((TILES, OBS, members), bf16),
            pltpu.VMEM((TILES, members, OBS), bf16),
            pltpu.VMEM((BLOCKS // 2, 6 * OBS, 2 * CELLS), bf16),
            pltpu.VMEM((members, cells), bf16),
            pltpu.VMEM((members * BLOCKS, CELLS), f32),
            pltpu.VMEM((turn * BLOCKS, CELLS), f32),
            pltpu.VMEM((TILES * OBS, CELLS), f32),
            pltpu.VMEM((members * BLOCKS, CELLS), bf16),
            pltpu.VMEM((OBS // half, members), bf16),
            pltpu.VMEM((OBS // half, members), bf16),
            pltpu.VMEM((ROUNDS, turn // half, OBS), bf16),
            pltpu.VMEM((ROUNDS, turn // half, OBS), bf16),
            dma,
            dma,
            dma,
            dma,
            dma((8 + max(half, 2),)),
            dma((TILES,)),
            dma((ROUNDS, 8 + max(half, 2))),
            dma((ROUNDS, TILES)),
            dma((2,)),
            dma((ROUNDS, 2)),
        ],
        compiler_params=pltpu.CompilerParams(
            collective_id=0, has_side_effects=True, vmem_limit_bytes=44 << 20
        ),
    )(
        taper_radius,
        predicted[0, 0],
        observation_jitter[0, 0],
        measured_value[0],
        measurement_variance[0],
        obs_block,
        taper_pattern.reshape(BLOCKS, PATTERN),
        params.reshape(members * BLOCKS, CELLS),
    )
    out = regrouped.reshape(cols, share, BLK_X, BLK_Y, CELLS).transpose(1, 2, 0, 3, 4)
    return out.reshape(share, BLK_X, cols * BLK_Y, CELLS)


def solution(mesh):
    placed = (
        P(None, "gx", "gy", None),
        P("gx", "gy", None, None),
        P("gx", "gy", None),
        P("gx", "gy", None),
        P("gx", "gy", None, None),
        P(),
        P("gx", "gy"),
        P("gx", "gy", None),
    )
    body = functools.partial(per_device, mesh.shape["gx"], mesh.shape["gy"])
    return jax.shard_map(
        body, mesh=mesh, in_specs=placed, out_specs=P("gy", "gx", None, None), check_vma=False
    )
```

```python
import functools

import jax
import jax.numpy as jnp
from jax import lax
from jax.experimental import pallas as pl
from jax.experimental.pallas import tpu as pltpu
from jax.sharding import PartitionSpec as P

CELLS = 128
BLK_X = 2
BLK_Y = 4
OBS = 128
PATTERN = 25
BLOCKS = BLK_X * BLK_Y
TILES = 9
UP, CENTRE, DOWN = 3, 4, 5
NEWTON = 9
PIECES = 6
ROUNDS = 3
MESH = pl.DeviceIdType.MESH
EXACT = lax.Precision.HIGHEST


def mm(a, b, precision=None):
    return jnp.dot(a, b, precision=precision, preferred_element_type=jnp.float32)


def newton_start(system, least):
    size = system.shape[0]
    most = jnp.max(jnp.sum(jnp.abs(system), axis=0, keepdims=True), axis=1, keepdims=True)
    scale = 2.0 / (most + least)
    spread = (most - least) / (most + least)
    eye = (
        lax.broadcasted_iota(jnp.int32, (size, size), 0)
        == lax.broadcasted_iota(jnp.int32, (size, size), 1)
    )
    return jnp.where(eye, 2.0 * scale, 0.0) - (scale * scale) * system, spread


def newton(system, inv, spread, steps):
    for _ in range(steps):
        square = spread * spread
        scale = 2.0 / (2.0 - square)
        spread = square / (2.0 - square)
        step = mm(inv, mm(system, inv, EXACT), EXACT)
        inv = (2.0 * scale) * inv - (scale * scale) * step
    return inv, spread


def kernel(
    rows,
    cols,
    radius_hbm,
    pred_hbm,
    jitter_hbm,
    value_hbm,
    var_hbm,
    map_hbm,
    pattern_hbm,
    params_hbm,
    recv_ref,
    radius_ref,
    pred_ref,
    jitter_ref,
    value_ref,
    var_ref,
    map_ref,
    pattern_ref,
    params_ref,
    d_ref,
    w_ref,
    gain_ref,
    anom_ref,
    wide_ref,
    delta_ref,
    taper_ref,
    sent_ref,
    d_near,
    d_far,
    w_near_first,
    w_far_first,
    w_near_rest,
    w_far_rest,
    load_sem,
    own_sem,
    all_send,
    all_recv,
    d_send,
    d_recv,
    w_send,
    w_recv,
    d_cross,
    w_cross,
):
    members = pred_ref.shape[0]
    piece = members // PIECES
    half = rows // 2
    share = members // cols
    gx = lax.axis_index("gx")
    gy = lax.axis_index("gy")
    lower = gx < half
    upper = gx >= half
    low_seam = gx == half - 1
    high_seam = gx == half
    seam = (gx == half - 1) | (gx == half)
    relay = jnp.logical_not(seam)
    not_low_seam = jnp.logical_not(low_seam)
    not_high_seam = jnp.logical_not(high_seam)
    column = lax.rem(gx, half)
    across = lax.rem(gx + half, rows)
    has_left = gy > 0
    has_right = gy < cols - 1
    sends_up = (gx > 0) & jnp.logical_not(high_seam)
    sends_down = (gx < rows - 1) & jnp.logical_not(low_seam)

    loads = [
        pltpu.make_async_copy(src, dst, load_sem.at[index])
        for index, (src, dst) in enumerate(
            (
                (pred_hbm, pred_ref),
                (var_hbm, var_ref),
                (map_hbm, map_ref),
                (jitter_hbm, jitter_ref),
                (value_hbm, value_ref),
                (radius_hbm, radius_ref),
                (pattern_hbm, pattern_ref),
                (params_hbm, params_ref),
            )
        )
    ]
    for load in loads:
        load.start()

    barrier = pltpu.get_barrier_semaphore()

    def greet(dev):
        pl.semaphore_signal(barrier, inc=1, device_id=dev, device_id_type=MESH)

    def greet_group(step, carry):
        greet((gx, lax.rem(gy + step, cols)))
        return carry

    lax.fori_loop(1, cols, greet_group, 0)
    greet((across, gy))

    @pl.when(sends_up)
    def _():
        greet((gx - 1, gy))

    @pl.when(sends_down)
    def _():
        greet((gx + 1, gy))

    for side, is_side, is_seam, at in (
        (0, lower, low_seam, half - 1),
        (half, upper, high_seam, half),
    ):

        @pl.when(is_side & relay)
        def _(at=at):
            greet((at, gy))

        @pl.when(is_seam)
        def _(side=side, at=at):
            for target in range(side, side + half):
                if target != at:
                    greet((target, gy))

    greetings = (
        cols
        + sends_up.astype(jnp.int32)
        + sends_down.astype(jnp.int32)
        + 1
        + (half - 2) * seam.astype(jnp.int32)
    )

    def remote(src, dst, send, recv, dev):
        return pltpu.make_async_remote_copy(
            src_ref=src,
            dst_ref=dst,
            send_sem=send,
            recv_sem=recv,
            device_id=dev,
            device_id_type=MESH,
        )

    def start(hops):
        for there, hop in hops:

            @pl.when(there)
            def _(hop=hop):
                hop.start()

    def wait_sent(hops):
        for there, hop in hops:

            @pl.when(there)
            def _(hop=hop):
                hop.wait_send()

    class Parcel:
        def __init__(self, buf, begin, size, send, recv):
            self.buf, self.begin, self.size, self.send, self.recv = buf, begin, size, send, recv

        def rows_of(self, slot):
            return self.buf.at[slot, pl.ds(self.begin, self.size), :]

        def hop(self, index, src, dst, dev):
            return remote(
                self.rows_of(src), self.rows_of(dst), self.send.at[index], self.recv.at[dst], dev
            )

        def own_hops(self):
            return (
                (sends_down, self.hop(0, CENTRE, UP, (gx + 1, gy))),
                (sends_up, self.hop(1, CENTRE, DOWN, (gx - 1, gy))),
                (has_right, self.hop(2, CENTRE, 1, (gx, gy + 1))),
                (has_left, self.hop(3, CENTRE, 7, (gx, gy - 1))),
            )

        def up_hops(self):
            return (
                (has_right, self.hop(4, UP, 0, (gx, gy + 1))),
                (has_left, self.hop(5, UP, 6, (gx, gy - 1))),
            )

        def down_hops(self):
            return (
                (has_right, self.hop(6, DOWN, 2, (gx, gy + 1))),
                (has_left, self.hop(7, DOWN, 8, (gx, gy - 1))),
            )

        def wait_slot(self, slot, there):
            @pl.when(there)
            def _():
                ref = self.rows_of(slot)
                pltpu.make_async_copy(ref, ref, self.recv.at[slot]).wait()

        def pass_on(self):
            self.wait_slot(UP, sends_up)
            self.wait_slot(DOWN, sends_down)
            start([(there & not_high_seam, hop) for there, hop in self.up_hops()])
            start([(there & not_low_seam, hop) for there, hop in self.down_hops()])

        def pass_on_seam(self):
            start([(there & high_seam, hop) for there, hop in self.up_hops()])
            start([(there & low_seam, hop) for there, hop in self.down_hops()])

        def wait_sides(self):
            for slot in (1, 0, 2):
                self.wait_slot(slot, has_left)
            for slot in (7, 6, 8):
                self.wait_slot(slot, has_right)

        def finish(self):
            wait_sent(self.own_hops())
            wait_sent(self.up_hops())
            wait_sent(self.down_hops())

    class Seam:
        def __init__(self, buf, begin, size, near, far, send, sems):
            self.buf, self.begin, self.size = buf, begin, size
            self.near, self.far, self.send = near, far, send
            self.near_sem, self.far_sem, self.slot_sem = sems.at[0], sems.at[1], sems.at[2]
            self.part = size // half

        def part_of(self, slot, index):
            offset = pl.multiple_of(self.begin + index * self.part, self.part)
            return self.buf.at[slot, pl.ds(offset, self.part), :]

        def out_hops(self):
            hops = []
            for side, is_seam, at in ((0, low_seam, half - 1), (half, high_seam, half)):
                for index in range(half):
                    if side + index == at:
                        dst, recv, dev = self.far, self.far_sem, (across, gy)
                    else:
                        dst, recv, dev = self.near, self.near_sem, (side + index, gy)
                    src = self.part_of(CENTRE, index)
                    hops.append((is_seam, remote(src, dst, self.send.at[index], recv, dev)))
            return hops

        def cross_hops(self):
            low_end, high_end = gx == 0, gx == rows - 1
            inner = relay & jnp.logical_not(low_end) & jnp.logical_not(high_end)
            send, dev = self.send.at[0], (across, gy)
            to_up, to_down = self.part_of(UP, 0), self.part_of(DOWN, half - 1)
            return (
                (inner, remote(self.near, self.far, send, self.far_sem, dev)),
                (low_end, remote(self.near, to_up, send, self.slot_sem, dev)),
                (high_end, remote(self.near, to_down, send, self.slot_sem, dev)),
            )

        def last_hops(self):
            hops = []
            for is_side, at, slot in ((lower, half - 1, DOWN), (upper, half, UP)):
                dst = self.part_of(slot, column)
                hop = remote(self.far, dst, self.send.at[1], self.slot_sem, (at, gy))
                hops.append((is_side & relay, hop))
            return hops

        def cross(self):
            @pl.when(relay)
            def _():
                pltpu.make_async_copy(self.near, self.near, self.near_sem).wait()

            start(self.cross_hops())

        def last(self):
            @pl.when(relay)
            def _():
                pltpu.make_async_copy(self.far, self.far, self.far_sem).wait()

            start(self.last_hops())

        def wait_slot(self):
            for is_seam, slot in ((high_seam, UP), (low_seam, DOWN)):

                @pl.when(is_seam)
                def _(slot=slot):
                    ref = self.buf.at[slot, pl.ds(self.begin, self.size), :]
                    pltpu.make_async_copy(ref, ref, self.slot_sem).wait()

        def finish(self):
            wait_sent(self.out_hops())
            wait_sent(self.cross_hops())
            wait_sent(self.last_hops())

    arrives = {UP: gx > 0, DOWN: gx < rows - 1}
    arrives.update({slot: has_left for slot in (0, 1, 2)})
    arrives.update({slot: has_right for slot in (6, 7, 8)})

    for slot, there in arrives.items():

        @pl.when(jnp.logical_not(there))
        def _(slot=slot):
            d_ref[slot] = jnp.zeros(d_ref.shape[1:], d_ref.dtype)
            w_ref[slot] = jnp.zeros(w_ref.shape[1:], w_ref.dtype)

    turn_size = 2 * piece
    d_parcel = Parcel(d_ref, 0, OBS, d_send, d_recv)
    w_parcels = [
        Parcel(w_ref, turn * turn_size, turn_size, w_send.at[turn], w_recv.at[turn])
        for turn in range(ROUNDS)
    ]
    d_seam = Seam(d_ref, 0, OBS, d_near, d_far, d_cross.at[0], d_cross.at[1])
    w_first = Seam(
        w_ref, 0, turn_size, w_near_first, w_far_first, w_cross.at[0], w_cross.at[1]
    )
    w_rest = Seam(
        w_ref,
        turn_size,
        members - turn_size,
        w_near_rest,
        w_far_rest,
        w_cross.at[2],
        w_cross.at[3],
    )

    loads[0].wait()
    pred = pred_ref[...]
    deviation = pred - jnp.sum(pred, axis=0, keepdims=True) / members
    d_own = deviation.astype(jnp.bfloat16)
    d_turned = deviation.T.astype(jnp.bfloat16)
    d_ref[CENTRE] = d_turned
    pl.semaphore_wait(barrier, greetings)
    start(d_seam.out_hops())
    start(d_parcel.own_hops())
    for load in loads[1:]:
        load.wait()

    gram = mm(d_turned, d_own) / (members - 1)
    own_map = jnp.broadcast_to(map_ref[gx, pl.ds(gy, 1), :].astype(jnp.float32), (OBS, OBS))
    eye = (
        lax.broadcasted_iota(jnp.int32, (OBS, OBS), 0)
        == lax.broadcasted_iota(jnp.int32, (OBS, OBS), 1)
    )
    variance = var_ref[...]
    system = jnp.where(own_map == own_map.T, gram, 0.0) + jnp.where(eye, variance, 0.0)
    inv, spread = newton_start(system, jnp.min(variance, axis=1, keepdims=True))
    inv, spread = newton(system, inv, spread, 6)
    d_seam.cross()
    inv, spread = newton(system, inv, spread, NEWTON - 6)
    deviation_scale = jnp.sqrt(variance)
    for turn in range(ROUNDS):
        for place, which in enumerate((turn, PIECES - 1 - turn)):
            who = slice(which * piece, (which + 1) * piece)
            residual = (
                value_ref[...] + deviation_scale * jitter_ref[who, :] - pred_ref[who, :]
            )
            at = (2 * turn + place) * piece
            w_ref[CENTRE, at : at + piece, :] = mm(residual, inv, EXACT).astype(jnp.bfloat16)
        if turn == 0:
            start(w_first.out_hops())
        if turn == ROUNDS - 1:
            start(w_rest.out_hops())
        start(w_parcels[turn].own_hops())

    d_parcel.pass_on()

    block = lax.broadcasted_iota(jnp.int32, (BLOCKS, OBS), 0)
    reach = jnp.zeros((BLOCKS, OBS), jnp.int32)
    for index in range(BLOCKS):
        reach = jnp.where(block == index, radius_ref[index // BLK_Y, index % BLK_Y] + 1, reach)
    reach = reach.astype(jnp.float32)
    reach = reach * reach
    listed = [
        jnp.broadcast_to(pattern_ref[:, slot : slot + 1], (BLOCKS, OBS)) for slot in range(PATTERN)
    ]
    for tile in range(TILES):
        at_x = lax.rem(gx + rows + tile % 3 - 1, rows)
        at_y = lax.rem(gy + cols + tile // 3 - 1, cols)
        near = jnp.broadcast_to(map_ref[at_x, pl.ds(at_y, 1), :], (BLOCKS, OBS))
        step_x = (tile % 3 - 1) * BLK_X + (near >> 2) - (block >> 2)
        step_y = (tile // 3 - 1) * BLK_Y + (near & 3) - (block & 3)
        inside = (jnp.abs(step_x) <= 2) & (jnp.abs(step_y) <= 2)
        offset = (step_x + 2) * 5 + (step_y + 2)
        picked = jnp.zeros((BLOCKS, OBS), jnp.int32)
        for slot in range(PATTERN):
            picked = jnp.where(offset == slot, listed[slot], picked)
        distance = (step_x * step_x + step_y * step_y).astype(jnp.float32)
        shaped = jnp.maximum(1.0 - distance / reach, 0.0)
        taper = jnp.where(inside, picked.astype(jnp.float32), 0.0) * shaped / (members - 1)
        filled = jnp.concatenate([taper, jnp.zeros((OBS - BLOCKS, OBS), jnp.float32)], axis=0)
        taper_ref[tile * OBS : (tile + 1) * OBS, :] = filled.T

    batch = 64

    def batch_rows(step):
        return pl.ds(pl.multiple_of(step * batch * BLOCKS, batch * BLOCKS), batch * BLOCKS)

    def batch_of(step):
        wide = params_ref[batch_rows(step), :].astype(jnp.float32)
        return wide.reshape(batch, BLOCKS, CELLS)

    mean = lax.fori_loop(
        0,
        members // batch,
        lambda step, total: total + jnp.sum(batch_of(step), axis=0),
        jnp.zeros((BLOCKS, CELLS), jnp.float32),
    ) * (1.0 / members)

    @pl.loop(0, members // batch)
    def _(step):
        centred = batch_of(step) - mean[None]
        wide_ref[batch_rows(step), :] = centred.reshape(batch * BLOCKS, CELLS)

    for index in range(BLOCKS):
        for first in range(0, members, 256):
            anom_ref[first : first + 256, index * CELLS : (index + 1) * CELLS] = wide_ref[
                pl.ds(first * BLOCKS + index, 256, stride=BLOCKS), :
            ].astype(jnp.bfloat16)

    near_tiles = 6
    obs = near_tiles * OBS

    def first_slot(group):
        return 3 * (group % 2)

    def gain_of(group):
        cells = slice(group * 2 * CELLS, (group + 1) * 2 * CELLS)
        first = first_slot(group)
        d_set = d_ref[first : first + near_tiles].reshape(obs, members)
        cross = mm(d_set, anom_ref[:, cells])
        weight = taper_ref[first * OBS : first * OBS + obs, :]
        for side in range(2):
            index = 2 * group + side
            gain_ref[group, :, side * CELLS : (side + 1) * CELLS] = (
                cross[:, side * CELLS : (side + 1) * CELLS] * weight[:, index : index + 1]
            ).astype(jnp.bfloat16)

    d_seam.last()
    w_first.cross()
    w_parcels[0].pass_on()
    w_rest.cross()
    w_first.last()
    d_seam.wait_slot()
    d_parcel.pass_on_seam()
    w_parcels[1].pass_on()
    w_parcels[2].pass_on()
    w_first.wait_slot()
    w_parcels[0].pass_on_seam()
    d_parcel.wait_sides()
    for group in range(BLOCKS // 2):
        gain_of(group)

    fan = cols // PIECES

    def send_rows(target):
        size = share * BLOCKS
        return sent_ref.at[pl.ds(pl.multiple_of(target * size, size), size), :]

    own_copy = pltpu.make_async_copy(send_rows(gy), recv_ref.at[gy], own_sem)
    far_side = lax.div(2 * gy, cols)

    def finish(turn):
        w_parcels[turn].wait_sides()
        who = slice(turn * turn_size, (turn + 1) * turn_size)
        for group in range(BLOCKS // 2):
            first = first_slot(group)
            w_set = jnp.concatenate(
                [w_ref[slot, who, :] for slot in range(first, first + near_tiles)], axis=1
            )
            delta = mm(w_set, gain_ref[group])
            for side in range(2):
                delta_ref[pl.ds(2 * group + side, 2 * piece, stride=BLOCKS), :] = delta[
                    :, side * CELLS : (side + 1) * CELLS
                ]
        size = piece * BLOCKS
        for place, which in enumerate((turn, PIECES - 1 - turn)):
            to = slice(which * size, (which + 1) * size)
            sent_ref[to, :] = (
                params_ref[to, :].astype(jnp.float32)
                + delta_ref[place * size : (place + 1) * size, :]
            ).astype(jnp.bfloat16)
        other, near = PIECES - 1 - turn, turn
        for which in (
            other + far_side * (near - other),
            near + far_side * (other - near),
        ):

            def send(step, carry, which=which):
                target = which * fan + lax.rem(step + gy, fan)

                @pl.when(target != gy)
                def _():
                    remote(
                        send_rows(target), recv_ref.at[gy], all_send, all_recv, (gx, target)
                    ).start()

                @pl.when(target == gy)
                def _():
                    own_copy.start()

                return carry

            lax.fori_loop(0, fan, send, 0)

    finish(0)
    w_rest.last()
    w_rest.wait_slot()
    w_parcels[1].pass_on_seam()
    w_parcels[2].pass_on_seam()
    finish(1)
    finish(2)

    others = recv_ref.at[pl.ds(0, cols - 1)]
    for parcel in (d_parcel, *w_parcels, d_seam, w_first, w_rest):
        parcel.finish()
    own_copy.wait()
    pltpu.make_async_copy(others, others, all_send).wait()
    pltpu.make_async_copy(others, others, all_recv).wait()


def per_device(
    rows,
    cols,
    params,
    predicted,
    measured_value,
    measurement_variance,
    observation_jitter,
    obs_block,
    taper_radius,
    taper_pattern,
):
    members = params.shape[0]
    share = members // cols
    half = rows // 2
    cells = BLOCKS * CELLS
    turn = members // ROUNDS
    hbm = pl.BlockSpec(memory_space=pltpu.HBM)
    dma = pltpu.SemaphoreType.DMA
    bf16, f32 = jnp.bfloat16, jnp.float32
    regrouped = pl.pallas_call(
        functools.partial(kernel, rows, cols),
        out_shape=jax.ShapeDtypeStruct((cols, share * BLOCKS, CELLS), bf16),
        in_specs=[hbm] * 8,
        out_specs=pl.BlockSpec(memory_space=pl.ANY),
        scratch_shapes=[
            pltpu.SMEM((BLK_X, BLK_Y), jnp.int32),
            pltpu.VMEM((members, OBS), f32),
            pltpu.VMEM((members, OBS), f32),
            pltpu.VMEM((1, OBS), f32),
            pltpu.VMEM((1, OBS), f32),
            pltpu.VMEM((rows, cols, OBS), jnp.int32),
            pltpu.VMEM((BLOCKS, PATTERN), jnp.int32),
            pltpu.VMEM((members * BLOCKS, CELLS), bf16),
            pltpu.VMEM((TILES, OBS, members), bf16),
            pltpu.VMEM((TILES, members, OBS), bf16),
            pltpu.VMEM((BLOCKS // 2, 6 * OBS, 2 * CELLS), bf16),
            pltpu.VMEM((members, cells), bf16),
            pltpu.VMEM((members * BLOCKS, CELLS), f32),
            pltpu.VMEM((turn * BLOCKS, CELLS), f32),
            pltpu.VMEM((TILES * OBS, CELLS), f32),
            pltpu.VMEM((members * BLOCKS, CELLS), bf16),
            pltpu.VMEM((OBS // half, members), bf16),
            pltpu.VMEM((OBS // half, members), bf16),
            pltpu.VMEM((turn // half, OBS), bf16),
            pltpu.VMEM((turn // half, OBS), bf16),
            pltpu.VMEM((2 * turn // half, OBS), bf16),
            pltpu.VMEM((2 * turn // half, OBS), bf16),
            dma((8,)),
            dma,
            dma,
            dma,
            dma((8,)),
            dma((TILES,)),
            dma((ROUNDS, 8)),
            dma((ROUNDS, TILES)),
            dma((2, max(half, 3))),
            dma((4, max(half, 3))),
        ],
        compiler_params=pltpu.CompilerParams(
            collective_id=0, has_side_effects=True, vmem_limit_bytes=56 << 20
        ),
    )(
        taper_radius,
        predicted[0, 0],
        observation_jitter[0, 0],
        measured_value[0],
        measurement_variance[0],
        obs_block,
        taper_pattern.reshape(BLOCKS, PATTERN),
        params.reshape(members * BLOCKS, CELLS),
    )
    out = regrouped.reshape(cols, share, BLK_X, BLK_Y, CELLS).transpose(1, 2, 0, 3, 4)
    return out.reshape(share, BLK_X, cols * BLK_Y, CELLS)


def solution(mesh):
    placed = (
        P(None, "gx", "gy", None),
        P("gx", "gy", None, None),
        P("gx", "gy", None),
        P("gx", "gy", None),
        P("gx", "gy", None, None),
        P(),
        P("gx", "gy"),
        P("gx", "gy", None),
    )
    body = functools.partial(per_device, mesh.shape["gx"], mesh.shape["gy"])
    return jax.shard_map(
        body, mesh=mesh, in_specs=placed, out_specs=P("gy", "gx", None, None), check_vma=False
    )
```

```python
import functools

import jax
import jax.numpy as jnp
from jax import lax
from jax.experimental import pallas as pl
from jax.experimental.pallas import tpu as pltpu
from jax.sharding import PartitionSpec as P

CELLS = 128
BLK_X = 2
BLK_Y = 4
OBS = 128
PATTERN = 25
BLOCKS = BLK_X * BLK_Y
TILES = 9
UP, CENTRE, DOWN = 3, 4, 5
NEWTON = 9
PIECES = 6
ROUNDS = 3
MESH = pl.DeviceIdType.MESH
EXACT = lax.Precision.HIGHEST


def mm(a, b, precision=None):
    return jnp.dot(a, b, precision=precision, preferred_element_type=jnp.float32)


def newton_start(system, least):
    size = system.shape[0]
    most = jnp.max(jnp.sum(jnp.abs(system), axis=0, keepdims=True), axis=1, keepdims=True)
    scale = 2.0 / (most + least)
    spread = (most - least) / (most + least)
    eye = (
        lax.broadcasted_iota(jnp.int32, (size, size), 0)
        == lax.broadcasted_iota(jnp.int32, (size, size), 1)
    )
    return jnp.where(eye, 2.0 * scale, 0.0) - (scale * scale) * system, spread


def newton(system, inv, spread, steps):
    for _ in range(steps):
        square = spread * spread
        scale = 2.0 / (2.0 - square)
        spread = square / (2.0 - square)
        step = mm(inv, mm(system, inv, EXACT), EXACT)
        inv = (2.0 * scale) * inv - (scale * scale) * step
    return inv, spread


def kernel(
    rows,
    cols,
    radius_hbm,
    pred_hbm,
    jitter_hbm,
    value_hbm,
    var_hbm,
    map_hbm,
    pattern_hbm,
    params_hbm,
    recv_ref,
    radius_ref,
    pred_ref,
    jitter_ref,
    value_ref,
    var_ref,
    map_ref,
    pattern_ref,
    params_ref,
    d_ref,
    w_ref,
    gain_ref,
    anom_ref,
    wide_ref,
    delta_ref,
    taper_ref,
    sent_ref,
    d_near,
    d_far,
    w_near_first,
    w_far_first,
    w_near_rest,
    w_far_rest,
    load_sem,
    own_sem,
    all_send,
    all_recv,
    d_send,
    d_recv,
    w_send,
    w_recv,
    d_cross,
    w_cross,
):
    members = pred_ref.shape[0]
    piece = members // PIECES
    half = rows // 2
    share = members // cols
    gx = lax.axis_index("gx")
    gy = lax.axis_index("gy")
    lower = gx < half
    upper = gx >= half
    low_seam = gx == half - 1
    high_seam = gx == half
    seam = (gx == half - 1) | (gx == half)
    relay = jnp.logical_not(seam)
    not_low_seam = jnp.logical_not(low_seam)
    not_high_seam = jnp.logical_not(high_seam)
    column = lax.rem(gx, half)
    across = lax.rem(gx + half, rows)
    has_left = gy > 0
    has_right = gy < cols - 1
    sends_up = (gx > 0) & jnp.logical_not(high_seam)
    sends_down = (gx < rows - 1) & jnp.logical_not(low_seam)

    loads = [
        pltpu.make_async_copy(src, dst, load_sem.at[index])
        for index, (src, dst) in enumerate(
            (
                (pred_hbm, pred_ref),
                (var_hbm, var_ref),
                (map_hbm, map_ref),
                (jitter_hbm, jitter_ref),
                (value_hbm, value_ref),
                (radius_hbm, radius_ref),
                (pattern_hbm, pattern_ref),
                (params_hbm, params_ref),
            )
        )
    ]
    for load in loads:
        load.start()

    barrier = pltpu.get_barrier_semaphore()

    def greet(dev):
        pl.semaphore_signal(barrier, inc=1, device_id=dev, device_id_type=MESH)

    def greet_group(step, carry):
        greet((gx, lax.rem(gy + step, cols)))
        return carry

    lax.fori_loop(1, cols, greet_group, 0)
    greet((across, gy))

    @pl.when(sends_up)
    def _():
        greet((gx - 1, gy))

    @pl.when(sends_down)
    def _():
        greet((gx + 1, gy))

    for side, is_side, is_seam, at in (
        (0, lower, low_seam, half - 1),
        (half, upper, high_seam, half),
    ):

        @pl.when(is_side & relay)
        def _(at=at):
            greet((at, gy))

        @pl.when(is_seam)
        def _(side=side, at=at):
            for target in range(side, side + half):
                if target != at:
                    greet((target, gy))

    greetings = (
        cols
        + sends_up.astype(jnp.int32)
        + sends_down.astype(jnp.int32)
        + 1
        + (half - 2) * seam.astype(jnp.int32)
    )

    def remote(src, dst, send, recv, dev):
        return pltpu.make_async_remote_copy(
            src_ref=src,
            dst_ref=dst,
            send_sem=send,
            recv_sem=recv,
            device_id=dev,
            device_id_type=MESH,
        )

    def start(hops):
        for there, hop in hops:

            @pl.when(there)
            def _(hop=hop):
                hop.start()

    def wait_sent(hops):
        for there, hop in hops:

            @pl.when(there)
            def _(hop=hop):
                hop.wait_send()

    class Parcel:
        def __init__(self, buf, begin, size, send, recv):
            self.buf, self.begin, self.size, self.send, self.recv = buf, begin, size, send, recv

        def rows_of(self, slot):
            return self.buf.at[slot, pl.ds(self.begin, self.size), :]

        def hop(self, index, src, dst, dev):
            return remote(
                self.rows_of(src), self.rows_of(dst), self.send.at[index], self.recv.at[dst], dev
            )

        def own_hops(self):
            return (
                (sends_down, self.hop(0, CENTRE, UP, (gx + 1, gy))),
                (sends_up, self.hop(1, CENTRE, DOWN, (gx - 1, gy))),
                (has_right, self.hop(2, CENTRE, 1, (gx, gy + 1))),
                (has_left, self.hop(3, CENTRE, 7, (gx, gy - 1))),
            )

        def up_hops(self):
            return (
                (has_right, self.hop(4, UP, 0, (gx, gy + 1))),
                (has_left, self.hop(5, UP, 6, (gx, gy - 1))),
            )

        def down_hops(self):
            return (
                (has_right, self.hop(6, DOWN, 2, (gx, gy + 1))),
                (has_left, self.hop(7, DOWN, 8, (gx, gy - 1))),
            )

        def wait_slot(self, slot, there):
            @pl.when(there)
            def _():
                ref = self.rows_of(slot)
                pltpu.make_async_copy(ref, ref, self.recv.at[slot]).wait()

        def pass_on(self):
            self.wait_slot(UP, sends_up)
            self.wait_slot(DOWN, sends_down)
            start([(there & not_high_seam, hop) for there, hop in self.up_hops()])
            start([(there & not_low_seam, hop) for there, hop in self.down_hops()])

        def pass_on_seam(self):
            start([(there & high_seam, hop) for there, hop in self.up_hops()])
            start([(there & low_seam, hop) for there, hop in self.down_hops()])

        def wait_sides(self):
            for slot in (1, 0, 2):
                self.wait_slot(slot, has_left)
            for slot in (7, 6, 8):
                self.wait_slot(slot, has_right)

        def finish(self):
            wait_sent(self.own_hops())
            wait_sent(self.up_hops())
            wait_sent(self.down_hops())

    class Seam:
        def __init__(self, buf, begin, size, near, far, send, sems):
            self.buf, self.begin, self.size = buf, begin, size
            self.near, self.far, self.send = near, far, send
            self.near_sem, self.far_sem, self.slot_sem = sems.at[0], sems.at[1], sems.at[2]
            self.part = size // half

        def part_of(self, slot, index):
            offset = pl.multiple_of(self.begin + index * self.part, self.part)
            return self.buf.at[slot, pl.ds(offset, self.part), :]

        def out_hops(self):
            hops = []
            for side, is_seam, at in ((0, low_seam, half - 1), (half, high_seam, half)):
                for index in range(half):
                    if side + index == at:
                        dst, recv, dev = self.far, self.far_sem, (across, gy)
                    else:
                        dst, recv, dev = self.near, self.near_sem, (side + index, gy)
                    src = self.part_of(CENTRE, index)
                    hops.append((is_seam, remote(src, dst, self.send.at[index], recv, dev)))
            return hops

        def cross_hops(self):
            low_end, high_end = gx == 0, gx == rows - 1
            inner = relay & jnp.logical_not(low_end) & jnp.logical_not(high_end)
            send, dev = self.send.at[0], (across, gy)
            to_up, to_down = self.part_of(UP, 0), self.part_of(DOWN, half - 1)
            return (
                (inner, remote(self.near, self.far, send, self.far_sem, dev)),
                (low_end, remote(self.near, to_up, send, self.slot_sem, dev)),
                (high_end, remote(self.near, to_down, send, self.slot_sem, dev)),
            )

        def last_hops(self):
            hops = []
            for is_side, at, slot in ((lower, half - 1, DOWN), (upper, half, UP)):
                dst = self.part_of(slot, column)
                hop = remote(self.far, dst, self.send.at[1], self.slot_sem, (at, gy))
                hops.append((is_side & relay, hop))
            return hops

        def cross(self):
            @pl.when(relay)
            def _():
                pltpu.make_async_copy(self.near, self.near, self.near_sem).wait()

            start(self.cross_hops())

        def last(self):
            @pl.when(relay)
            def _():
                pltpu.make_async_copy(self.far, self.far, self.far_sem).wait()

            start(self.last_hops())

        def wait_slot(self):
            for is_seam, slot in ((high_seam, UP), (low_seam, DOWN)):

                @pl.when(is_seam)
                def _(slot=slot):
                    ref = self.buf.at[slot, pl.ds(self.begin, self.size), :]
                    pltpu.make_async_copy(ref, ref, self.slot_sem).wait()

        def finish(self):
            wait_sent(self.out_hops())
            wait_sent(self.cross_hops())
            wait_sent(self.last_hops())

    arrives = {UP: gx > 0, DOWN: gx < rows - 1}
    arrives.update({slot: has_left for slot in (0, 1, 2)})
    arrives.update({slot: has_right for slot in (6, 7, 8)})

    for slot, there in arrives.items():

        @pl.when(jnp.logical_not(there))
        def _(slot=slot):
            d_ref[slot] = jnp.zeros(d_ref.shape[1:], d_ref.dtype)
            w_ref[slot] = jnp.zeros(w_ref.shape[1:], w_ref.dtype)

    turn_size = 2 * piece
    d_parcel = Parcel(d_ref, 0, OBS, d_send, d_recv)
    w_parcels = [
        Parcel(w_ref, turn * turn_size, turn_size, w_send.at[turn], w_recv.at[turn])
        for turn in range(ROUNDS)
    ]
    d_seam = Seam(d_ref, 0, OBS, d_near, d_far, d_cross.at[0], d_cross.at[1])
    w_first = Seam(
        w_ref, 0, turn_size, w_near_first, w_far_first, w_cross.at[0], w_cross.at[1]
    )
    w_rest = Seam(
        w_ref,
        turn_size,
        members - turn_size,
        w_near_rest,
        w_far_rest,
        w_cross.at[2],
        w_cross.at[3],
    )

    loads[0].wait()
    pred = pred_ref[...]
    deviation = pred - jnp.sum(pred, axis=0, keepdims=True) / members
    d_own = deviation.astype(jnp.bfloat16)
    d_turned = deviation.T.astype(jnp.bfloat16)
    d_ref[CENTRE] = d_turned
    for load in loads[1:]:
        load.wait()

    gram = mm(d_turned, d_own) / (members - 1)
    own_map = jnp.broadcast_to(map_ref[gx, pl.ds(gy, 1), :].astype(jnp.float32), (OBS, OBS))
    eye = (
        lax.broadcasted_iota(jnp.int32, (OBS, OBS), 0)
        == lax.broadcasted_iota(jnp.int32, (OBS, OBS), 1)
    )
    variance = var_ref[...]
    system = jnp.where(own_map == own_map.T, gram, 0.0) + jnp.where(eye, variance, 0.0)
    inv, spread = newton_start(system, jnp.min(variance, axis=1, keepdims=True))
    inv, _ = newton(system, inv, spread, NEWTON)
    deviation_scale = jnp.sqrt(variance)
    for turn in range(ROUNDS):
        for place, which in enumerate((turn, PIECES - 1 - turn)):
            who = slice(which * piece, (which + 1) * piece)
            residual = (
                value_ref[...] + deviation_scale * jitter_ref[who, :] - pred_ref[who, :]
            )
            at = (2 * turn + place) * piece
            w_ref[CENTRE, at : at + piece, :] = mm(residual, inv, EXACT).astype(jnp.bfloat16)

    pl.semaphore_wait(barrier, greetings)
    start(d_seam.out_hops())
    start(w_first.out_hops())
    start(d_parcel.own_hops())
    start(w_parcels[0].own_hops())
    start(w_rest.out_hops())
    start(w_parcels[1].own_hops())
    start(w_parcels[2].own_hops())

    block = lax.broadcasted_iota(jnp.int32, (BLOCKS, OBS), 0)
    reach = jnp.zeros((BLOCKS, OBS), jnp.int32)
    for index in range(BLOCKS):
        reach = jnp.where(block == index, radius_ref[index // BLK_Y, index % BLK_Y] + 1, reach)
    reach = reach.astype(jnp.float32)
    reach = reach * reach
    listed = [
        jnp.broadcast_to(pattern_ref[:, slot : slot + 1], (BLOCKS, OBS)) for slot in range(PATTERN)
    ]
    for tile in range(TILES):
        at_x = lax.rem(gx + rows + tile % 3 - 1, rows)
        at_y = lax.rem(gy + cols + tile // 3 - 1, cols)
        near = jnp.broadcast_to(map_ref[at_x, pl.ds(at_y, 1), :], (BLOCKS, OBS))
        step_x = (tile % 3 - 1) * BLK_X + (near >> 2) - (block >> 2)
        step_y = (tile // 3 - 1) * BLK_Y + (near & 3) - (block & 3)
        inside = (jnp.abs(step_x) <= 2) & (jnp.abs(step_y) <= 2)
        offset = (step_x + 2) * 5 + (step_y + 2)
        picked = jnp.zeros((BLOCKS, OBS), jnp.int32)
        for slot in range(PATTERN):
            picked = jnp.where(offset == slot, listed[slot], picked)
        distance = (step_x * step_x + step_y * step_y).astype(jnp.float32)
        shaped = jnp.maximum(1.0 - distance / reach, 0.0)
        taper = jnp.where(inside, picked.astype(jnp.float32), 0.0) * shaped / (members - 1)
        filled = jnp.concatenate([taper, jnp.zeros((OBS - BLOCKS, OBS), jnp.float32)], axis=0)
        taper_ref[tile * OBS : (tile + 1) * OBS, :] = filled.T

    batch = 64

    def batch_rows(step):
        return pl.ds(pl.multiple_of(step * batch * BLOCKS, batch * BLOCKS), batch * BLOCKS)

    def batch_of(step):
        wide = params_ref[batch_rows(step), :].astype(jnp.float32)
        return wide.reshape(batch, BLOCKS, CELLS)

    mean = lax.fori_loop(
        0,
        members // batch,
        lambda step, total: total + jnp.sum(batch_of(step), axis=0),
        jnp.zeros((BLOCKS, CELLS), jnp.float32),
    ) * (1.0 / members)

    @pl.loop(0, members // batch)
    def _(step):
        centred = batch_of(step) - mean[None]
        wide_ref[batch_rows(step), :] = centred.reshape(batch * BLOCKS, CELLS)

    for index in range(BLOCKS):
        for first in range(0, members, 256):
            anom_ref[first : first + 256, index * CELLS : (index + 1) * CELLS] = wide_ref[
                pl.ds(first * BLOCKS + index, 256, stride=BLOCKS), :
            ].astype(jnp.bfloat16)

    near_tiles = 6
    obs = near_tiles * OBS

    def first_slot(group):
        return 3 * (group % 2)

    def gain_of(group):
        cells = slice(group * 2 * CELLS, (group + 1) * 2 * CELLS)
        first = first_slot(group)
        d_set = d_ref[first : first + near_tiles].reshape(obs, members)
        cross = mm(d_set, anom_ref[:, cells])
        weight = taper_ref[first * OBS : first * OBS + obs, :]
        for side in range(2):
            index = 2 * group + side
            gain_ref[group, :, side * CELLS : (side + 1) * CELLS] = (
                cross[:, side * CELLS : (side + 1) * CELLS] * weight[:, index : index + 1]
            ).astype(jnp.bfloat16)

    d_seam.cross()
    w_first.cross()
    d_parcel.pass_on()
    w_rest.cross()
    w_parcels[0].pass_on()
    d_seam.last()
    w_first.last()
    d_seam.wait_slot()
    d_parcel.pass_on_seam()
    w_parcels[1].pass_on()
    w_parcels[2].pass_on()
    w_first.wait_slot()
    w_parcels[0].pass_on_seam()
    d_parcel.wait_sides()
    for group in range(BLOCKS // 2):
        gain_of(group)

    fan = cols // PIECES

    def send_rows(target):
        size = share * BLOCKS
        return sent_ref.at[pl.ds(pl.multiple_of(target * size, size), size), :]

    own_copy = pltpu.make_async_copy(send_rows(gy), recv_ref.at[gy], own_sem)
    far_side = lax.div(2 * gy, cols)

    def finish(turn):
        w_parcels[turn].wait_sides()
        who = slice(turn * turn_size, (turn + 1) * turn_size)
        for group in range(BLOCKS // 2):
            first = first_slot(group)
            w_set = jnp.concatenate(
                [w_ref[slot, who, :] for slot in range(first, first + near_tiles)], axis=1
            )
            delta = mm(w_set, gain_ref[group])
            for side in range(2):
                delta_ref[pl.ds(2 * group + side, 2 * piece, stride=BLOCKS), :] = delta[
                    :, side * CELLS : (side + 1) * CELLS
                ]
        size = piece * BLOCKS
        for place, which in enumerate((turn, PIECES - 1 - turn)):
            to = slice(which * size, (which + 1) * size)
            sent_ref[to, :] = (
                params_ref[to, :].astype(jnp.float32)
                + delta_ref[place * size : (place + 1) * size, :]
            ).astype(jnp.bfloat16)
        other, near = PIECES - 1 - turn, turn
        for which in (
            other + far_side * (near - other),
            near + far_side * (other - near),
        ):

            def send(step, carry, which=which):
                target = which * fan + lax.rem(step + gy, fan)

                @pl.when(target != gy)
                def _():
                    remote(
                        send_rows(target), recv_ref.at[gy], all_send, all_recv, (gx, target)
                    ).start()

                @pl.when(target == gy)
                def _():
                    own_copy.start()

                return carry

            lax.fori_loop(0, fan, send, 0)

    finish(0)
    w_rest.last()
    w_rest.wait_slot()
    w_parcels[1].pass_on_seam()
    w_parcels[2].pass_on_seam()
    finish(1)
    finish(2)

    others = recv_ref.at[pl.ds(0, cols - 1)]
    for parcel in (d_parcel, *w_parcels, d_seam, w_first, w_rest):
        parcel.finish()
    own_copy.wait()
    pltpu.make_async_copy(others, others, all_send).wait()
    pltpu.make_async_copy(others, others, all_recv).wait()


def per_device(
    rows,
    cols,
    params,
    predicted,
    measured_value,
    measurement_variance,
    observation_jitter,
    obs_block,
    taper_radius,
    taper_pattern,
):
    members = params.shape[0]
    share = members // cols
    half = rows // 2
    cells = BLOCKS * CELLS
    turn = members // ROUNDS
    hbm = pl.BlockSpec(memory_space=pltpu.HBM)
    dma = pltpu.SemaphoreType.DMA
    bf16, f32 = jnp.bfloat16, jnp.float32
    regrouped = pl.pallas_call(
        functools.partial(kernel, rows, cols),
        out_shape=jax.ShapeDtypeStruct((cols, share * BLOCKS, CELLS), bf16),
        in_specs=[hbm] * 8,
        out_specs=pl.BlockSpec(memory_space=pl.ANY),
        scratch_shapes=[
            pltpu.SMEM((BLK_X, BLK_Y), jnp.int32),
            pltpu.VMEM((members, OBS), f32),
            pltpu.VMEM((members, OBS), f32),
            pltpu.VMEM((1, OBS), f32),
            pltpu.VMEM((1, OBS), f32),
            pltpu.VMEM((rows, cols, OBS), jnp.int32),
            pltpu.VMEM((BLOCKS, PATTERN), jnp.int32),
            pltpu.VMEM((members * BLOCKS, CELLS), bf16),
            pltpu.VMEM((TILES, OBS, members), bf16),
            pltpu.VMEM((TILES, members, OBS), bf16),
            pltpu.VMEM((BLOCKS // 2, 6 * OBS, 2 * CELLS), bf16),
            pltpu.VMEM((members, cells), bf16),
            pltpu.VMEM((members * BLOCKS, CELLS), f32),
            pltpu.VMEM((turn * BLOCKS, CELLS), f32),
            pltpu.VMEM((TILES * OBS, CELLS), f32),
            pltpu.VMEM((members * BLOCKS, CELLS), bf16),
            pltpu.VMEM((OBS // half, members), bf16),
            pltpu.VMEM((OBS // half, members), bf16),
            pltpu.VMEM((turn // half, OBS), bf16),
            pltpu.VMEM((turn // half, OBS), bf16),
            pltpu.VMEM((2 * turn // half, OBS), bf16),
            pltpu.VMEM((2 * turn // half, OBS), bf16),
            dma((8,)),
            dma,
            dma,
            dma,
            dma((8,)),
            dma((TILES,)),
            dma((ROUNDS, 8)),
            dma((ROUNDS, TILES)),
            dma((2, max(half, 3))),
            dma((4, max(half, 3))),
        ],
        compiler_params=pltpu.CompilerParams(
            collective_id=0, has_side_effects=True, vmem_limit_bytes=56 << 20
        ),
    )(
        taper_radius,
        predicted[0, 0],
        observation_jitter[0, 0],
        measured_value[0],
        measurement_variance[0],
        obs_block,
        taper_pattern.reshape(BLOCKS, PATTERN),
        params.reshape(members * BLOCKS, CELLS),
    )
    out = regrouped.reshape(cols, share, BLK_X, BLK_Y, CELLS).transpose(1, 2, 0, 3, 4)
    return out.reshape(share, BLK_X, cols * BLK_Y, CELLS)


def solution(mesh):
    placed = (
        P(None, "gx", "gy", None),
        P("gx", "gy", None, None),
        P("gx", "gy", None),
        P("gx", "gy", None),
        P("gx", "gy", None, None),
        P(),
        P("gx", "gy"),
        P("gx", "gy", None),
    )
    body = functools.partial(per_device, mesh.shape["gx"], mesh.shape["gy"])
    return jax.shard_map(
        body, mesh=mesh, in_specs=placed, out_specs=P("gy", "gx", None, None), check_vma=False
    )
```
